32 devices in a mesh: dp: 2 (over core), ctx: 16 (over z, y, x).
Axes of the slice: x: 2, y: 2, z: 4, core: 2. Of those that a mesh axis runs over, the one named last changes fastest.
Arguments:
- features: bfloat16 [2, 4096, 6144], P('dp', 'ctx'), may hold values from -6 to 6
- short_w: float32 [3, 6144], replicated, may hold values from -3.5 to 3.5
- long_h: float32 [128, 128], replicated, may hold values from -0.5 to 0.5
- skip_bias: float32 [2048], replicated, may hold values from -1 to 1
- cotangent: bfloat16 [2, 4096, 2048], P('dp', 'ctx'), may hold values from -6 to 6
Outputs:
- output: bfloat16 [2, 4096, 2048], P('dp', 'ctx')
- grad_features: bfloat16 [2, 4096, 6144], P('dp', 'ctx')
- grad_short: float32 [3, 6144], replicated
- grad_long: float32 [128, 128], replicated
- grad_skip: float32 [2048], replicated
The draws below stay inside these ranges and needn't reach their ends.
All inputs are finite; a program needn't handle non-finite values.
Results may differ from the reference program's by a relative error of at most 0.008.
Values may be sent and summed in bfloat16 or wider, within the bound.
A program may use at most 128 MiB of HBM per device.

```python
import math
import jax
import jax.numpy as jnp
from jax import lax

C = 2048
LF = 128
BLK = 32
SEQ = 4096
SEQS = 2
G = 128


def level_of(stream_key, shape, split, low, high):
    def one(position, parts):
        steps = jax.random.uniform(jax.random.fold_in(jax.random.fold_in(stream_key, 6), position), (parts,), jnp.float32, low / len(split), high / len(split))
        return jnp.repeat(jnp.exp(steps), shape[position] // parts).reshape((-1,) + (1,) * (len(shape) - position - 1))

    level = one(*split[0])
    for cut in split[1:]:
        level = level * one(*cut)
    return level


def scatter_about(rng, extent, spread, reach, cuts=(), kind=jnp.bfloat16):
    level = level_of(rng, extent, cuts, -0.22, 0.18) if cuts else 1.0
    drawn = jax.random.normal(rng, extent, jnp.float32) * spread * level
    return jnp.minimum(jnp.maximum(drawn, -reach), reach).astype(kind)


def setup_inputs(seed: int = 0) -> dict:
    key_of = jax.random.split(jax.random.key(seed), 6)
    return {
        "features": scatter_about(key_of[0], (SEQS, SEQ, 3 * C), 1.0, 6.0, ((0, 2), (1, 16))),
        "short_w": scatter_about(key_of[1], (3, 3 * C), 3 ** -0.5, 3.5, (), jnp.float32),
        "long_h": scatter_about(key_of[2], (G, LF), LF ** -0.5, 0.5, (), jnp.float32),
        "skip_bias": jnp.clip(jax.random.uniform(key_of[3], (C,), jnp.float32, -1.0, 1.0), -1.0, 1.0),
        "cotangent": scatter_about(key_of[4], (SEQS, SEQ, C), 1.0, 6.0, ((0, 2), (1, 16))),
    }


def banded(filters, block, adjoint):
    groups, taps = filters.shape
    width = block + taps - 1
    row_index = lax.broadcasted_iota(jnp.int32, (block, width), 0)
    col_index = lax.broadcasted_iota(jnp.int32, (block, width), 1)
    if adjoint:
        lag = col_index - row_index
    else:
        lag = taps - 1 - (col_index - row_index)
    inside = (lag >= 0) & (lag < taps)
    picked = jnp.take(filters, jnp.clip(lag, 0, taps - 1), axis=1)
    return jnp.where(inside[None], picked, jnp.zeros((), filters.dtype))


def windows(extended, block, taps):
    count = (extended.shape[0] - taps + 1) // block
    padded = jnp.concatenate([extended, jnp.zeros((1, extended.shape[1]), extended.dtype)], axis=0)
    blocked = padded.reshape(count + taps // block, block, -1)
    pieces = [blocked[start:start + count] for start in range(taps // block + 1)]
    return jnp.concatenate(pieces, axis=1)[:, : block + taps - 1]


def grouped(array, groups):
    return array.reshape(array.shape[:-1] + (array.shape[-1] // groups, groups))


def diagonal_sums(products, taps):
    groups, block, width = products.shape
    flat = products.reshape(groups, block * width)
    flat = jnp.concatenate([flat, jnp.zeros((groups, block), products.dtype)], axis=1)
    flat = flat.reshape(groups, block, width + 1)
    return jnp.sum(flat[:, :, :taps], axis=1)[:, ::-1]


def split_count(count):
    return math.gcd(count, 16)


def mixed_conv(matrix, window, groups):
    count, width, channels = window.shape
    pieces = split_count(count)
    parted = window.reshape(pieces, count // pieces, width, channels)

    def one_piece(part):
        result = jnp.einsum("gts,bsig->btig", matrix, grouped(part.astype(jnp.float32), groups),
                            precision=lax.Precision.HIGHEST)
        return result.reshape(part.shape[0] * matrix.shape[1], channels)

    return lax.map(one_piece, parted).reshape(count * matrix.shape[1], channels)


def filter_products(grad_blocks, window, groups):
    count = window.shape[0]
    pieces = split_count(count)
    grad_parts = grad_blocks.reshape((pieces, count // pieces) + grad_blocks.shape[1:])
    win_parts = window.reshape((pieces, count // pieces) + window.shape[1:])

    def one_piece(pair):
        grad_part, win_part = pair
        return jnp.einsum("btig,bsig->gts", grouped(grad_part.astype(jnp.float32), groups),
                          grouped(win_part.astype(jnp.float32), groups),
                          precision=lax.Precision.HIGHEST)

    return jnp.sum(lax.map(one_piece, (grad_parts, win_parts)), axis=0)


def reference(features, short_w, long_h, skip_bias, cotangent):
    groups, taps = long_h.shape
    channels = skip_bias.shape[0]
    forward_mat = banded(long_h.astype(jnp.bfloat16), BLK, False).astype(jnp.float32)
    adjoint_mat = banded(long_h.astype(jnp.bfloat16), BLK, True).astype(jnp.float32)
    outputs = []
    grads_in = []
    grad_long = jnp.zeros((groups, taps), jnp.float32)
    grad_skip = jnp.zeros((channels,), jnp.float32)
    grad_short = jnp.zeros((3, 3 * channels), jnp.float32)
    for seq_index in range(SEQS):
        inputs_f = features[seq_index].astype(jnp.float32)
        padded_in = jnp.pad(inputs_f, ((2, 0), (0, 0)))
        featured = short_w[0] * inputs_f + short_w[1] * padded_in[1:-1] + short_w[2] * padded_in[:-2]
        queries = featured[:, :channels]
        keys = featured[:, channels:2 * channels]
        values = featured[:, 2 * channels:]
        z_loc = (keys * values).astype(jnp.bfloat16)
        z_ext = jnp.concatenate([jnp.zeros((taps - 1, channels), jnp.bfloat16), z_loc], axis=0)
        z_win = windows(z_ext, BLK, taps)
        z_f = z_loc.astype(jnp.float32)
        mixed = mixed_conv(forward_mat, z_win, groups) + skip_bias * z_f
        outputs.append((queries * mixed).astype(jnp.bfloat16))
        upstream = cotangent[seq_index].astype(jnp.float32)
        grad_q = upstream * mixed
        grad_mix = (upstream * queries).astype(jnp.bfloat16)
        grad_ext = jnp.concatenate([grad_mix, jnp.zeros((taps - 1, channels), jnp.bfloat16)], axis=0)
        grad_mix_f = grad_mix.astype(jnp.float32)
        grad_z = mixed_conv(adjoint_mat, windows(grad_ext, BLK, taps), groups) + skip_bias * grad_mix_f
        grad_feat = jnp.concatenate([grad_q, grad_z * values, grad_z * keys], axis=1).astype(jnp.bfloat16)
        grad_feat_f = grad_feat.astype(jnp.float32)
        padded_grad = jnp.pad(grad_feat_f, ((0, 2), (0, 0)))
        grad_in = short_w[0] * grad_feat_f + short_w[1] * padded_grad[1:-1] + short_w[2] * padded_grad[2:]
        grads_in.append(grad_in.astype(jnp.bfloat16))
        count = grad_mix.shape[0] // BLK
        products = filter_products(grad_mix.reshape(count, BLK, channels), z_win, groups)
        grad_long = grad_long + diagonal_sums(products, taps)
        grad_skip = grad_skip + jnp.sum(grad_mix_f * z_f, axis=0)
        grad_short = grad_short + jnp.stack([
            jnp.sum(grad_feat_f * inputs_f, axis=0),
            jnp.sum(grad_feat_f * padded_in[1:-1], axis=0),
            jnp.sum(grad_feat_f * padded_in[:-2], axis=0)])
    scale = (SEQS * SEQ) ** -0.5
    return (jnp.stack(outputs), jnp.stack(grads_in), grad_short * scale, grad_long * scale, grad_skip * scale)
```

```python
import functools

import jax
import jax.numpy as jnp
from jax import lax
from jax.experimental import pallas as pl
from jax.experimental.pallas import tpu as pltpu
from jax.sharding import PartitionSpec as P

LANES = 128
PITCH = 132


def delayed(tile, edge, by):
    row = lax.broadcasted_iota(jnp.int32, tile.shape, 0)
    moved = pltpu.roll(tile, by, 0)
    if by == 1:
        return jnp.where(row == 0, edge[1:2], moved)
    return jnp.where(row == 0, edge[0:1], jnp.where(row == 1, edge[1:2], moved))


def advanced(tile, by):
    rows = tile.shape[0]
    row = lax.broadcasted_iota(jnp.int32, tile.shape, 0)
    return jnp.where(row < rows - by, pltpu.roll(tile, rows - by, 0), 0.0)


def filtered(feat_ref, w_ref, cols, edge, first, count):
    w = w_ref[:, cols]
    tile = feat_ref[first : first + count, cols].astype(jnp.float32)
    return w[0:1] * tile + w[1:2] * delayed(tile, edge, 1) + w[2:3] * delayed(tile, edge, 2)


def turned_tile(i):
    return pl.ds(i * PITCH, LANES)


def turned_rows(channels):
    return channels // LANES * PITCH


def column_tile(stream, i, channels):
    return pl.ds(pl.multiple_of(stream * channels + i * LANES, LANES), LANES)


def halo_kernel(
    span, feat_ref, last_ref, cot_ref, w_ref, zt, gt, edge_ref,
    z_send, g_send, z_rim, g_rim, edge_got, sems,
):
    rows = feat_ref.shape[0]
    parts = z_send.shape[0]
    channels = parts * LANES
    blocks = rows // LANES
    f32, bf16 = jnp.float32, jnp.bfloat16
    length = span[1]
    dp, ctx = lax.axis_index("dp"), lax.axis_index("ctx")
    after, before = (dp, (ctx + 1) % length), (dp, (ctx + length - 1) % length)
    has_before = jnp.where(ctx > 0, 1.0, 0.0).astype(f32)
    has_after = jnp.where(ctx + 1 < length, 1.0, 0.0).astype(f32)

    def send(source, target, index, device):
        copy = pltpu.make_async_remote_copy(
            src_ref=source, dst_ref=target, send_sem=sems.at[index], recv_sem=sems.at[index + 1],
            device_id=device, device_id_type=pl.DeviceIdType.MESH,
        )
        copy.start()
        return copy

    barrier = pltpu.get_barrier_semaphore()
    for peer in (after, before):
        pl.semaphore_signal(barrier, inc=1, device_id=peer, device_id_type=pl.DeviceIdType.MESH)
    pl.semaphore_wait(barrier, 2)
    edge_copy = send(last_ref, edge_got, 0, after)

    def z_tail(i, _):
        pair = []
        for stream in (1, 2):
            cols = column_tile(stream, i, channels)
            edge = feat_ref[rows - LANES - 8 : rows - LANES, cols].astype(f32)[6:8]
            pair.append(filtered(feat_ref, w_ref, cols, edge, rows - LANES, LANES))
        z_send[i] = (pair[0] * pair[1]).astype(bf16)
        return 0

    lax.fori_loop(0, parts, z_tail, 0)
    z_copy = send(z_send, z_rim, 2, after)
    edge_copy.wait()
    edge_ref[...] = edge_got[...].astype(f32) * has_before

    def g_head(i, _):
        own = column_tile(0, i, channels)
        queries = filtered(feat_ref, w_ref, own, edge_ref[:, own], 0, LANES)
        g_send[i] = (cot_ref[:LANES, own].astype(f32) * queries).astype(bf16)
        return 0

    lax.fori_loop(0, parts, g_head, 0)
    g_copy = send(g_send, g_rim, 4, before)

    def featurize(i, _):
        own = column_tile(0, i, channels)
        made = []
        for stream in range(3):
            cols = column_tile(stream, i, channels)
            made.append(filtered(feat_ref, w_ref, cols, edge_ref[:, cols], 0, rows))
        z = (made[1] * made[2]).astype(bf16).astype(f32)
        g = (cot_ref[:, own].astype(f32) * made[0]).astype(bf16).astype(f32)
        for n in range(blocks):
            zt[n + 1, turned_tile(i)] = z[n * LANES : (n + 1) * LANES].T
            gt[n, turned_tile(i)] = g[n * LANES : (n + 1) * LANES].T
        return 0

    lax.fori_loop(0, parts, featurize, 0)
    z_copy.wait()
    g_copy.wait()

    def turn_rims(i, _):
        own = turned_tile(i)
        zt[0, own] = (z_rim[i].astype(f32) * has_before).T
        gt[blocks, own] = (g_rim[i].astype(f32) * has_after).T
        return 0

    lax.fori_loop(0, parts, turn_rims, 0)


def exchange(feat, cot, short_w):
    rows, wide = feat.shape
    channels = wide // 3
    parts = channels // LANES
    blocks = rows // LANES
    f32, bf16 = jnp.float32, jnp.bfloat16
    span = (lax.axis_size("dp"), lax.axis_size("ctx"))
    vmem = pl.BlockSpec(memory_space=pltpu.VMEM)
    rim = pltpu.VMEM((parts, LANES, LANES), bf16)
    turned = jax.ShapeDtypeStruct((blocks + 1, turned_rows(channels), LANES), f32)
    return pl.pallas_call(
        functools.partial(halo_kernel, span),
        out_shape=(turned, turned, jax.ShapeDtypeStruct((2, wide), f32)),
        in_specs=[vmem] * 4,
        out_specs=(vmem,) * 3,
        scratch_shapes=[
            rim, rim, rim, rim, pltpu.VMEM((2, wide), bf16), pltpu.SemaphoreType.DMA((6,)),
        ],
        compiler_params=pltpu.CompilerParams(collective_id=1, has_side_effects=True),
    )(feat, feat[rows - 2 :], cot, short_w)


def local_kernel(
    feat_ref, edge_ref, cot_ref, zt, gt, w_ref, h_ref, skip_ref,
    out_ref, gin_ref, head_ref, tail_ref, sums_ref,
    mt, gzt, lags,
):
    rows, channels = cot_ref.shape
    parts = channels // LANES
    groups = h_ref.shape[0]
    blocks = rows // LANES
    f32, bf16 = jnp.float32, jnp.bfloat16

    s_index = lax.broadcasted_iota(jnp.int32, (LANES, LANES), 0)
    t_index = lax.broadcasted_iota(jnp.int32, (LANES, LANES), 1)
    causal = t_index >= s_index

    def convolve(g, _):
        picked = pl.ds(g, parts, stride=PITCH)
        zs = [zt[n, picked].astype(bf16) for n in range(blocks + 1)]
        gs = [gt[n, picked].astype(bf16) for n in range(blocks + 1)]
        z_win = jnp.concatenate(
            [jnp.concatenate([zs[n], zs[n + 1]], axis=1) for n in range(blocks)], axis=0
        )
        g_win = jnp.concatenate(
            [jnp.concatenate([gs[n], gs[n + 1]], axis=1) for n in range(blocks)], axis=0
        )
        g_own = jnp.concatenate(gs[:blocks], axis=0)
        taps = jnp.broadcast_to(h_ref[pl.ds(g, 1), :].astype(bf16).astype(f32), (LANES, LANES))
        circ = pltpu.roll(taps, 0, 1, stride=1, stride_axis=0)
        t0 = jnp.where(causal, circ, 0.0).astype(bf16)
        t1 = jnp.where(causal, 0.0, circ).astype(bf16)
        mixed = jnp.dot(z_win, jnp.concatenate([t1, t0], axis=0), preferred_element_type=f32)
        back = lax.dot_general(
            g_win, jnp.concatenate([t0, t1], axis=1), (((1,), (1,)), ((), ())),
            preferred_element_type=f32,
        )
        for n in range(blocks):
            mt[n, picked] = mixed[n * parts : (n + 1) * parts]
            gzt[n, picked] = back[n * parts : (n + 1) * parts]
        prod = lax.dot_general(z_win, g_own, (((0,), (0,)), ((), ())), preferred_element_type=f32)
        kept = jnp.where(causal, prod[LANES:], prod[:LANES])
        total = kept[:8]
        for low in range(8, LANES, 8):
            total = total + pltpu.roll(kept[low : low + 8], LANES - low, 1)
        lags[pl.ds(g, 8, stride=groups)] = total
        return 0

    lax.fori_loop(0, groups, convolve, 0, unroll=8)
    total = lags[:groups]
    for low in range(1, 8):
        total = total + pltpu.roll(lags[low * groups : (low + 1) * groups], LANES - low, 1)
    sums_ref[:groups] = total

    def finish(i, _):
        own = column_tile(0, i, channels)
        made = []
        for stream in range(3):
            cols = column_tile(stream, i, channels)
            made.append(filtered(feat_ref, w_ref, cols, edge_ref[:, cols], 0, rows))
        q, k, v = made
        z = (k * v).astype(bf16).astype(f32)
        g = (cot_ref[:, own].astype(f32) * q).astype(bf16).astype(f32)
        sums_ref[pl.ds(groups + i, 1), :] = jnp.sum(z * g, axis=0, keepdims=True)
        skip = skip_ref[:, own]
        mixed = jnp.concatenate([mt[n, turned_tile(i)].T for n in range(blocks)], axis=0) + skip * z
        grad_z = jnp.concatenate([gzt[n, turned_tile(i)].T for n in range(blocks)], axis=0) + skip * g
        out_ref[:, own] = (q * mixed).astype(bf16)
        grads = [cot_ref[:, own].astype(f32) * mixed, grad_z * v, grad_z * k]
        for stream in range(3):
            cols = column_tile(stream, i, channels)
            grad = grads[stream].astype(bf16).astype(f32)
            tile = feat_ref[:, cols].astype(f32)
            edge = edge_ref[:, cols]
            w = w_ref[:, cols]
            total = w[0:1] * grad + w[1:2] * advanced(grad, 1) + w[2:3] * advanced(grad, 2)
            gin_ref[:, cols] = total.astype(bf16)
            tail_ref[:, cols] = total[rows - 8 :]
            head_ref[:, cols] = grad[:2]
            for tap in range(3):
                past = delayed(tile, edge, tap) if tap else tile
                slot = groups + parts + (tap * 3 + stream) * parts + i
                sums_ref[pl.ds(slot, 1), :] = jnp.sum(grad * past, axis=0, keepdims=True)
        return 0

    lax.fori_loop(0, parts, finish, 0)
    used = groups + 10 * parts
    if used < sums_ref.shape[0]:
        sums_ref[used:] = jnp.zeros((sums_ref.shape[0] - used, LANES), f32)


def local_work(feat, edge, cot, zt, gt, short_w, filters, skip, sums):
    rows, wide = feat.shape
    channels = wide // 3
    blocks = rows // LANES
    f32, bf16 = jnp.float32, jnp.bfloat16
    vmem = pl.BlockSpec(memory_space=pltpu.VMEM)
    return pl.pallas_call(
        local_kernel,
        out_shape=(
            jax.ShapeDtypeStruct((rows, channels), bf16),
            jax.ShapeDtypeStruct((rows, wide), bf16),
            jax.ShapeDtypeStruct((2, wide), f32),
            jax.ShapeDtypeStruct((8, wide), f32),
            jax.ShapeDtypeStruct((sums, LANES), f32),
        ),
        in_specs=[vmem] * 8,
        out_specs=(vmem,) * 5,
        scratch_shapes=[
            pltpu.VMEM((blocks, turned_rows(channels), LANES), f32),
            pltpu.VMEM((blocks, turned_rows(channels), LANES), f32),
            pltpu.VMEM((8 * filters.shape[0], LANES), f32),
        ],
    )(feat, edge, cot, zt, gt, short_w, filters, skip)


INNER = 4


def sum_kernel(
    share, scale, span, sums_ref, head_ref, out_ref, ahead_ref,
    got_near, got_far, part, full, ahead,
    near_send, near_recv, far_send, far_recv, far_send2, far_recv2, near_send2, near_recv2, edge_sems,
):
    dp, ctx = lax.axis_index("dp"), lax.axis_index("ctx")
    dps, length = span
    near, far = dps * INNER, length // INNER
    outer, inner = ctx // INNER, ctx % INNER
    mine = dp * INNER + inner
    wide = far * share

    def near_peer(step):
        other = (mine + step) % near
        return other, (other // INNER, outer * INNER + other % INNER)

    def far_peer(step):
        other = (outer + step) % far
        return other, (dp, other * INNER + inner)

    def send(source, target, sems, device):
        copy = pltpu.make_async_remote_copy(
            src_ref=source, dst_ref=target, send_sem=sems[0], recv_sem=sems[1],
            device_id=device, device_id_type=pl.DeviceIdType.MESH,
        )
        copy.start()
        return copy

    after, before = (dp, (ctx + 1) % length), (dp, (ctx + length - 1) % length)
    peers = [near_peer(step)[1] for step in range(1, near)]
    peers += [far_peer(step)[1] for step in range(1, far)] + [after, before]
    barrier = pltpu.get_barrier_semaphore()
    for peer in peers:
        pl.semaphore_signal(barrier, inc=1, device_id=peer, device_id_type=pl.DeviceIdType.MESH)
    pl.semaphore_wait(barrier, len(peers))

    copies = []
    for step in range(1, near):
        other, device = near_peer(step)
        copies.append(send(
            sums_ref.at[pl.ds(other * wide, wide)], got_near.at[step - 1],
            (near_send.at[step - 1], near_recv.at[step - 1]), device,
        ))
    edge_copy = send(head_ref, ahead, (edge_sems.at[0], edge_sems.at[1]), before)
    total = sums_ref[pl.ds(mine * wide, wide)]
    for step, copy in enumerate(copies):
        copy.wait()
        total = total + got_near[step]
    part[...] = total

    copies = []
    for step in range(1, far):
        other, device = far_peer(step)
        copies.append(send(
            part.at[pl.ds(other * share, share)], got_far.at[step - 1],
            (far_send.at[step - 1], far_recv.at[step - 1]), device,
        ))
    total = part[pl.ds(outer * share, share)]
    for step, copy in enumerate(copies):
        copy.wait()
        total = total + got_far[step]
    place = pl.ds(mine * wide + outer * share, share)
    full[place] = total * scale

    copies = [
        send(
            full.at[place], full.at[place],
            (far_send2.at[step - 1], far_recv2.at[step - 1]), far_peer(step)[1],
        )
        for step in range(1, far)
    ]
    for copy in copies:
        copy.wait()
    place = pl.ds(mine * wide, wide)
    copies = [
        send(
            full.at[place], full.at[place],
            (near_send2.at[step - 1], near_recv2.at[step - 1]), near_peer(step)[1],
        )
        for step in range(1, near)
    ]
    for copy in copies:
        copy.wait()
    edge_copy.wait()
    out_ref[...] = full[...]
    ahead_ref[...] = ahead[...]


def total_over_devices(sums, head, share, scale):
    f32 = jnp.float32
    span = (lax.axis_size("dp"), lax.axis_size("ctx"))
    near, far = span[0] * INNER, span[1] // INNER
    rows = sums.shape[0]
    vmem = pl.BlockSpec(memory_space=pltpu.VMEM)
    dma = pltpu.SemaphoreType.DMA
    totals, ahead = pl.pallas_call(
        functools.partial(sum_kernel, share, scale, span),
        out_shape=(
            jax.ShapeDtypeStruct((rows, 1, LANES), f32),
            jax.ShapeDtypeStruct(head.shape, head.dtype),
        ),
        in_specs=[vmem] * 2,
        out_specs=(vmem,) * 2,
        scratch_shapes=[
            pltpu.VMEM((near - 1, far * share, 1, LANES), f32),
            pltpu.VMEM((max(far - 1, 1), share, 1, LANES), f32),
            pltpu.VMEM((far * share, 1, LANES), f32),
            pltpu.VMEM((rows, 1, LANES), f32),
            pltpu.VMEM(head.shape, head.dtype),
            dma((near - 1,)), dma((near - 1,)),
            dma((max(far - 1, 1),)), dma((max(far - 1, 1),)),
            dma((max(far - 1, 1),)), dma((max(far - 1, 1),)),
            dma((near - 1,)), dma((near - 1,)),
            dma((2,)),
        ],
        compiler_params=pltpu.CompilerParams(
            collective_id=0, has_side_effects=True, vmem_limit_bytes=16 * 1024 * 1024
        ),
    )(sums.reshape(rows, 1, LANES), head)
    return totals.reshape(rows, LANES), ahead


def body(features, short_w, long_h, skip_bias, cotangent):
    f32, bf16 = jnp.float32, jnp.bfloat16
    feat = features[0]
    cot = cotangent[0]
    rows = feat.shape[0]
    channels = skip_bias.shape[0]
    groups, taps = long_h.shape
    zt, gt, edge = exchange(feat, cot, short_w)
    devices = lax.axis_size("dp") * lax.axis_size("ctx")
    used = groups + 10 * (channels // LANES)
    share = -(-used // devices)
    output, grad_in, head, last, sums = local_work(
        feat, edge, cot, zt, gt, short_w, long_h, skip_bias[None], share * devices
    )
    scale = (devices * rows) ** (-0.5)
    totals, ahead = total_over_devices(sums, head, share, scale)
    ahead = jnp.where(lax.axis_index("ctx") + 1 < lax.axis_size("ctx"), ahead, 0.0)
    row0 = last[6] + short_w[2] * ahead[0]
    row1 = last[7] + short_w[1] * ahead[0] + short_w[2] * ahead[1]
    grad_in = lax.dynamic_update_slice(
        grad_in, jnp.stack([row0, row1]).astype(bf16), (rows - 2, 0)
    )
    parts = channels // LANES
    return (
        output[None],
        grad_in[None],
        totals[groups + parts : used].reshape(short_w.shape),
        totals[:groups],
        totals[groups : groups + parts].reshape(channels),
    )


def solution(mesh):
    return jax.shard_map(
        body,
        mesh=mesh,
        in_specs=(P("dp", "ctx", None), P(), P(), P(), P("dp", "ctx", None)),
        out_specs=(P("dp", "ctx", None), P("dp", "ctx", None), P(), P(), P()),
        check_vma=False,
    )
```

```python
import functools

import jax
import jax.numpy as jnp
from jax import lax
from jax.experimental import pallas as pl
from jax.experimental.pallas import tpu as pltpu
from jax.sharding import PartitionSpec as P

LANES = 128
PITCH = 132


def delayed(tile, edge, by):
    row = lax.broadcasted_iota(jnp.int32, tile.shape, 0)
    moved = pltpu.roll(tile, by, 0)
    if by == 1:
        return jnp.where(row == 0, edge[1:2], moved)
    return jnp.where(row == 0, edge[0:1], jnp.where(row == 1, edge[1:2], moved))


def filtered(feat_ref, w_ref, cols, edge, first, count):
    w = w_ref[:, cols]
    tile = feat_ref[first : first + count, cols].astype(jnp.float32)
    return w[0:1] * tile + w[1:2] * delayed(tile, edge, 1) + w[2:3] * delayed(tile, edge, 2)


def turned_tile(i):
    return pl.ds(i * PITCH, LANES)


def turned_rows(channels):
    return channels // LANES * PITCH


def column_tile(stream, i, channels):
    return pl.ds(pl.multiple_of(stream * channels + i * LANES, LANES), LANES)


def diagonals(kept):
    total = kept[:8]
    for low in range(8, LANES, 8):
        total = total + pltpu.roll(kept[low : low + 8], LANES - low, 1)
    return total


def main_kernel(
    span, feat_hbm, cot_hbm, w_ref, h_ref, skip_ref,
    out_ref, gin_ref, head_ref, tail_ref, sums_ref,
    feat_ref, cot_ref, staged, made, grads, zt, gt, rims, mt, gzt, t1_all, lags,
    z_send, g_send, z_rim, g_rim, edge_send, edge_got, edge_ref, sems, load_sems,
):
    rows, channels = cot_ref.shape
    parts = channels // LANES
    groups = h_ref.shape[0]
    blocks = rows // LANES
    f32, bf16 = jnp.float32, jnp.bfloat16
    length = span[1]
    dp, ctx = lax.axis_index("dp"), lax.axis_index("ctx")
    after, before = (dp, (ctx + 1) % length), (dp, (ctx + length - 1) % length)
    has_before = jnp.where(ctx > 0, 1.0, 0.0).astype(f32)
    has_after = jnp.where(ctx + 1 < length, 1.0, 0.0).astype(f32)

    early = rows - LANES - 16
    loads = []
    for source, target in (
        (feat_hbm.at[early:, channels:], feat_ref.at[early:, channels:]),
        (feat_hbm.at[:, :channels], feat_ref.at[:, :channels]),
        (cot_hbm, cot_ref),
        (feat_hbm.at[:early, channels:], feat_ref.at[:early, channels:]),
    ):
        copy = pltpu.make_async_copy(source, target, load_sems.at[len(loads)])
        copy.start()
        loads.append(copy)

    def send(source, target, index, device):
        copy = pltpu.make_async_remote_copy(
            src_ref=source, dst_ref=target, send_sem=sems.at[index], recv_sem=sems.at[index + 1],
            device_id=device, device_id_type=pl.DeviceIdType.MESH,
        )
        copy.start()
        return copy

    barrier = pltpu.get_barrier_semaphore()
    for peer in (after, before):
        pl.semaphore_signal(barrier, inc=1, device_id=peer, device_id_type=pl.DeviceIdType.MESH)

    loads[0].wait()
    loads[1].wait()
    edge_send[...] = feat_ref[rows - 16 :, :].astype(f32)[14:16].astype(bf16)
    pl.semaphore_wait(barrier, 2)
    edge_copy = send(edge_send, edge_got, 0, after)

    def z_tail(i, _):
        pair = []
        for stream in (1, 2):
            cols = column_tile(stream, i, channels)
            edge = feat_ref[early : early + 16, cols].astype(f32)[14:16]
            pair.append(filtered(feat_ref, w_ref, cols, edge, rows - LANES, LANES))
        z_send[i] = (pair[0] * pair[1]).astype(bf16)
        return 0

    half = parts // 2
    copies = []
    for n in range(2):
        piece = pl.ds(n * half, half)
        lax.fori_loop(n * half, (n + 1) * half, z_tail, 0)
        copies.append(send(z_send.at[piece], z_rim.at[piece], 2 + 2 * n, after))
    edge_copy.wait()
    edge_ref[...] = edge_got[...].astype(f32) * has_before
    loads[2].wait()

    def g_head(i, _):
        own = column_tile(0, i, channels)
        queries = filtered(feat_ref, w_ref, own, edge_ref[:, own], 0, LANES)
        g_send[i] = (cot_ref[:LANES, own].astype(f32) * queries).astype(bf16)
        return 0

    for n in range(2):
        piece = pl.ds(n * half, half)
        lax.fori_loop(n * half, (n + 1) * half, g_head, 0)
        copies.append(send(g_send.at[piece], g_rim.at[piece], 6 + 2 * n, before))
    loads[3].wait()

    def featurize(i, _):
        own = column_tile(0, i, channels)
        for stream in range(3):
            cols = column_tile(stream, i, channels)
            slot = stream * parts + i
            w = w_ref[:, cols]
            staged[slot, 6:8] = edge_ref[:, cols]
            staged[slot, 8:] = feat_ref[:, cols].astype(f32)
            made[slot] = (
                w[0:1] * staged[slot, 8 : 8 + rows]
                + w[1:2] * staged[slot, 7 : 7 + rows]
                + w[2:3] * staged[slot, 6 : 6 + rows]
            )
        total = jnp.zeros((1, LANES), f32)
        for n in range(blocks):
            at = pl.ds(n * LANES, LANES)
            z = (made[parts + i, at] * made[2 * parts + i, at]).astype(bf16).astype(f32)
            g = (cot_ref[at, own].astype(f32) * made[i, at]).astype(bf16).astype(f32)
            total = total + jnp.sum(z * g, axis=0, keepdims=True)
            zt[n, turned_tile(i)] = z.T
            gt[n, turned_tile(i)] = g.T
        sums_ref[pl.ds(groups + i, 1), :] = total
        return 0

    lax.fori_loop(0, parts, featurize, 0)

    s_index = lax.broadcasted_iota(jnp.int32, (LANES, LANES), 0)
    t_index = lax.broadcasted_iota(jnp.int32, (LANES, LANES), 1)
    causal = t_index >= s_index
    contract = lambda a, b, da, db: lax.dot_general(
        a, b, (((da,), (db,)), ((), ())), preferred_element_type=f32
    )

    def convolve(g, _):
        picked = pl.ds(g, parts, stride=PITCH)
        zs = [zt[n, picked].astype(bf16) for n in range(blocks)]
        gs = [gt[n, picked].astype(bf16) for n in range(blocks)]
        none = jnp.zeros((parts, LANES), bf16)
        z_win = jnp.concatenate(
            [jnp.concatenate([a, b], axis=1) for a, b in zip([none] + zs, zs)], axis=0
        )
        g_win = jnp.concatenate(
            [jnp.concatenate([a, b], axis=1) for a, b in zip(gs, gs[1:] + [none])], axis=0
        )
        taps = jnp.broadcast_to(h_ref[pl.ds(g, 1), :].astype(bf16).astype(f32), (LANES, LANES))
        circ = pltpu.roll(taps, 0, 1, stride=1, stride_axis=0)
        t0 = jnp.where(causal, circ, 0.0).astype(bf16)
        t1 = jnp.where(causal, 0.0, circ).astype(bf16)
        t1_all[pl.ds(pl.multiple_of(g * LANES, LANES), LANES)] = t1
        mixed = contract(z_win, jnp.concatenate([t1, t0], axis=0), 1, 0)
        back = contract(g_win, jnp.concatenate([t0, t1], axis=1), 1, 1)
        for n in range(blocks):
            mt[n, picked] = mixed[n * parts : (n + 1) * parts]
            gzt[n, picked] = back[n * parts : (n + 1) * parts]
        prod = contract(z_win, jnp.concatenate(gs, axis=0), 0, 0)
        kept = jnp.where(causal, prod[LANES:], prod[:LANES])
        lags[pl.ds(g, 8, stride=PITCH)] = diagonals(kept)
        return 0

    lax.fori_loop(0, groups, convolve, 0, unroll=8)
    for copy in copies:
        copy.wait()

    def turn_rims(i, _):
        rims[0, turned_tile(i)] = (z_rim[i].astype(f32) * has_before).T
        rims[1, turned_tile(i)] = (g_rim[i].astype(f32) * has_after).T
        return 0

    lax.fori_loop(0, parts, turn_rims, 0, unroll=2)

    def convolve_rims(g, _):
        picked = pl.ds(g, parts, stride=PITCH)
        zr = rims[0, picked].astype(bf16)
        gr = rims[1, picked].astype(bf16)
        t1 = t1_all[pl.ds(pl.multiple_of(g * LANES, LANES), LANES)]
        mt[0, picked] += contract(zr, t1, 1, 0)
        gzt[blocks - 1, picked] += contract(gr, t1, 1, 1)
        prod = contract(zr, gt[0, picked].astype(bf16), 0, 0)
        lags[pl.ds(g, 8, stride=PITCH)] += diagonals(jnp.where(causal, 0.0, prod))
        return 0

    lax.fori_loop(0, groups, convolve_rims, 0, unroll=8)
    total = lags[:groups]
    for low in range(1, 8):
        total = total + pltpu.roll(lags[low * PITCH : low * PITCH + groups], LANES - low, 1)
    sums_ref[:groups] = total
    grads[:, rows:] = jnp.zeros((3, 8, LANES), f32)

    def finish(i, _):
        own = column_tile(0, i, channels)
        skip = skip_ref[:, own]
        for n in range(blocks):
            at = pl.ds(n * LANES, LANES)
            q, k, v = made[i, at], made[parts + i, at], made[2 * parts + i, at]
            ct = cot_ref[at, own].astype(f32)
            z = (k * v).astype(bf16).astype(f32)
            g = (ct * q).astype(bf16).astype(f32)
            mixed = mt[n, turned_tile(i)].T + skip * z
            grad_z = gzt[n, turned_tile(i)].T + skip * g
            out_ref[at, own] = (q * mixed).astype(bf16)
            grads[0, at] = (ct * mixed).astype(bf16).astype(f32)
            grads[1, at] = (grad_z * v).astype(bf16).astype(f32)
            grads[2, at] = (grad_z * k).astype(bf16).astype(f32)
        for stream in range(3):
            cols = column_tile(stream, i, channels)
            slot = stream * parts + i
            w = w_ref[:, cols]
            totals = [jnp.zeros((1, LANES), f32) for _ in range(3)]
            for n in range(blocks):
                low = n * LANES
                grad = grads[stream, low : low + LANES]
                new = (
                    w[0:1] * grad
                    + w[1:2] * grads[stream, low + 1 : low + 1 + LANES]
                    + w[2:3] * grads[stream, low + 2 : low + 2 + LANES]
                )
                gin_ref[low : low + LANES, cols] = new.astype(bf16)
                for tap in range(3):
                    past = staged[slot, 8 - tap + low : 8 - tap + low + LANES]
                    totals[tap] = totals[tap] + jnp.sum(grad * past, axis=0, keepdims=True)
            tail_ref[:, cols] = new[LANES - 8 :]
            head_ref[:, cols] = grads[stream, 0:2]
            for tap in range(3):
                line = groups + parts + (tap * 3 + stream) * parts + i
                sums_ref[pl.ds(line, 1), :] = totals[tap]
        return 0

    lax.fori_loop(0, parts, finish, 0)
    used = groups + 10 * parts
    if used < sums_ref.shape[0]:
        sums_ref[used:] = jnp.zeros((sums_ref.shape[0] - used, LANES), f32)


def main_work(feat, cot, short_w, filters, skip, sums):
    rows, wide = feat.shape
    channels = wide // 3
    parts = channels // LANES
    blocks = rows // LANES
    groups = filters.shape[0]
    f32, bf16 = jnp.float32, jnp.bfloat16
    span = (lax.axis_size("dp"), lax.axis_size("ctx"))
    vmem = pl.BlockSpec(memory_space=pltpu.VMEM)
    hbm = pl.BlockSpec(memory_space=pl.ANY)
    rim = pltpu.VMEM((parts, LANES, LANES), bf16)
    turned = pltpu.VMEM((blocks, turned_rows(channels), LANES), f32)
    return pl.pallas_call(
        functools.partial(main_kernel, span),
        out_shape=(
            jax.ShapeDtypeStruct((rows, channels), bf16),
            jax.ShapeDtypeStruct((rows, wide), bf16),
            jax.ShapeDtypeStruct((2, wide), f32),
            jax.ShapeDtypeStruct((8, wide), f32),
            jax.ShapeDtypeStruct((sums, LANES), f32),
        ),
        in_specs=[hbm, hbm, vmem, vmem, vmem],
        out_specs=(vmem,) * 5,
        scratch_shapes=[
            pltpu.VMEM((rows, wide), bf16),
            pltpu.VMEM((rows, channels), bf16),
            pltpu.VMEM((3 * parts, rows + 8, LANES), f32),
            pltpu.VMEM((3 * parts, rows, LANES), f32),
            pltpu.VMEM((3, rows + 8, LANES), f32),
            turned, turned,
            pltpu.VMEM((2, turned_rows(channels), LANES), f32),
            turned, turned,
            pltpu.VMEM((groups * LANES, LANES), bf16),
            pltpu.VMEM((8 * PITCH, LANES), f32),
            rim, rim, rim, rim,
            pltpu.VMEM((2, wide), bf16), pltpu.VMEM((2, wide), bf16), pltpu.VMEM((2, wide), f32),
            pltpu.SemaphoreType.DMA((10,)), pltpu.SemaphoreType.DMA((4,)),
        ],
        compiler_params=pltpu.CompilerParams(
            collective_id=1, has_side_effects=True, vmem_limit_bytes=60 * 1024 * 1024
        ),
    )(feat, cot, short_w, filters, skip)


INNER = 4


def sum_kernel(
    share, scale, span, sums_ref, head_ref, out_ref, ahead_ref,
    got_near, got_far, part, full, ahead,
    near_send, near_recv, far_send, far_recv, far_send2, far_recv2, near_send2, near_recv2, edge_sems,
):
    dp, ctx = lax.axis_index("dp"), lax.axis_index("ctx")
    dps, length = span
    near, far = dps * INNER, length // INNER
    outer, inner = ctx // INNER, ctx % INNER
    mine = dp * INNER + inner
    wide = far * share

    def near_peer(step):
        other = (mine + step) % near
        return other, (other // INNER, outer * INNER + other % INNER)

    def far_peer(step):
        other = (outer + step) % far
        return other, (dp, other * INNER + inner)

    def send(source, target, sems, device):
        copy = pltpu.make_async_remote_copy(
            src_ref=source, dst_ref=target, send_sem=sems[0], recv_sem=sems[1],
            device_id=device, device_id_type=pl.DeviceIdType.MESH,
        )
        copy.start()
        return copy

    after, before = (dp, (ctx + 1) % length), (dp, (ctx + length - 1) % length)
    peers = [near_peer(step)[1] for step in range(1, near)]
    peers += [far_peer(step)[1] for step in range(1, far)] + [after, before]
    barrier = pltpu.get_barrier_semaphore()
    for peer in peers:
        pl.semaphore_signal(barrier, inc=1, device_id=peer, device_id_type=pl.DeviceIdType.MESH)
    pl.semaphore_wait(barrier, len(peers))

    copies = []
    for step in range(1, near):
        other, device = near_peer(step)
        copies.append(send(
            sums_ref.at[pl.ds(other * wide, wide)], got_near.at[step - 1],
            (near_send.at[step - 1], near_recv.at[step - 1]), device,
        ))
    edge_copy = send(head_ref, ahead, (edge_sems.at[0], edge_sems.at[1]), before)
    total = sums_ref[pl.ds(mine * wide, wide)]
    for step, copy in enumerate(copies):
        copy.wait()
        total = total + got_near[step]
    part[...] = total

    copies = []
    for step in range(1, far):
        other, device = far_peer(step)
        copies.append(send(
            part.at[pl.ds(other * share, share)], got_far.at[step - 1],
            (far_send.at[step - 1], far_recv.at[step - 1]), device,
        ))
    total = part[pl.ds(outer * share, share)]
    for step, copy in enumerate(copies):
        copy.wait()
        total = total + got_far[step]
    place = pl.ds(mine * wide + outer * share, share)
    full[place] = total * scale

    copies = [
        send(
            full.at[place], full.at[place],
            (far_send2.at[step - 1], far_recv2.at[step - 1]), far_peer(step)[1],
        )
        for step in range(1, far)
    ]
    for copy in copies:
        copy.wait()
    place = pl.ds(mine * wide, wide)
    copies = [
        send(
            full.at[place], full.at[place],
            (near_send2.at[step - 1], near_recv2.at[step - 1]), near_peer(step)[1],
        )
        for step in range(1, near)
    ]
    for copy in copies:
        copy.wait()
    edge_copy.wait()
    out_ref[...] = full[...]
    ahead_ref[...] = ahead[...]


def total_over_devices(sums, head, share, scale):
    f32 = jnp.float32
    span = (lax.axis_size("dp"), lax.axis_size("ctx"))
    near, far = span[0] * INNER, span[1] // INNER
    rows = sums.shape[0]
    vmem = pl.BlockSpec(memory_space=pltpu.VMEM)
    dma = pltpu.SemaphoreType.DMA
    totals, ahead = pl.pallas_call(
        functools.partial(sum_kernel, share, scale, span),
        out_shape=(
            jax.ShapeDtypeStruct((rows, 1, LANES), f32),
            jax.ShapeDtypeStruct(head.shape, head.dtype),
        ),
        in_specs=[vmem] * 2,
        out_specs=(vmem,) * 2,
        scratch_shapes=[
            pltpu.VMEM((near - 1, far * share, 1, LANES), f32),
            pltpu.VMEM((max(far - 1, 1), share, 1, LANES), f32),
            pltpu.VMEM((far * share, 1, LANES), f32),
            pltpu.VMEM((rows, 1, LANES), f32),
            pltpu.VMEM(head.shape, head.dtype),
            dma((near - 1,)), dma((near - 1,)),
            dma((max(far - 1, 1),)), dma((max(far - 1, 1),)),
            dma((max(far - 1, 1),)), dma((max(far - 1, 1),)),
            dma((near - 1,)), dma((near - 1,)),
            dma((2,)),
        ],
        compiler_params=pltpu.CompilerParams(
            collective_id=0, has_side_effects=True, vmem_limit_bytes=16 * 1024 * 1024
        ),
    )(sums.reshape(rows, 1, LANES), head)
    return totals.reshape(rows, LANES), ahead


def body(features, short_w, long_h, skip_bias, cotangent):
    f32, bf16 = jnp.float32, jnp.bfloat16
    feat = features[0]
    cot = cotangent[0]
    rows = feat.shape[0]
    channels = skip_bias.shape[0]
    groups, taps = long_h.shape
    devices = lax.axis_size("dp") * lax.axis_size("ctx")
    used = groups + 10 * (channels // LANES)
    share = -(-used // devices)
    output, grad_in, head, last, sums = main_work(
        feat, cot, short_w, long_h, skip_bias[None], share * devices
    )
    scale = (devices * rows) ** (-0.5)
    totals, ahead = total_over_devices(sums, head, share, scale)
    ahead = jnp.where(lax.axis_index("ctx") + 1 < lax.axis_size("ctx"), ahead, 0.0)
    row0 = last[6] + short_w[2] * ahead[0]
    row1 = last[7] + short_w[1] * ahead[0] + short_w[2] * ahead[1]
    grad_in = lax.dynamic_update_slice(
        grad_in, jnp.stack([row0, row1]).astype(bf16), (rows - 2, 0)
    )
    parts = channels // LANES
    return (
        output[None],
        grad_in[None],
        totals[groups + parts : used].reshape(short_w.shape),
        totals[:groups],
        totals[groups : groups + parts].reshape(channels),
    )


def solution(mesh):
    return jax.shard_map(
        body,
        mesh=mesh,
        in_specs=(P("dp", "ctx", None), P(), P(), P(), P("dp", "ctx", None)),
        out_specs=(P("dp", "ctx", None), P("dp", "ctx", None), P(), P(), P()),
        check_vma=False,
    )
```

```python
import functools

import jax
import jax.numpy as jnp
from jax import lax
from jax.experimental import pallas as pl
from jax.experimental.pallas import tpu as pltpu
from jax.sharding import PartitionSpec as P

LANES = 128
PITCH = 132
INNER = 4
VMEM_LIMIT = 48 * 1024 * 1024


def delayed(tile, edge, by):
    row = lax.broadcasted_iota(jnp.int32, tile.shape, 0)
    moved = pltpu.roll(tile, by, 0)
    if by == 1:
        return jnp.where(row == 0, edge[1:2], moved)
    return jnp.where(row == 0, edge[0:1], jnp.where(row == 1, edge[1:2], moved))


def filtered(feat_ref, w_ref, cols, edge, first, count):
    w = w_ref[:, cols]
    tile = feat_ref[first : first + count, cols].astype(jnp.float32)
    return w[0:1] * tile + w[1:2] * delayed(tile, edge, 1) + w[2:3] * delayed(tile, edge, 2)


def turned_tile(i):
    return pl.ds(i * PITCH, LANES)


def turned_rows(channels):
    return channels // LANES * PITCH


def column_tile(stream, i, channels):
    return pl.ds(pl.multiple_of(stream * channels + i * LANES, LANES), LANES)


def diagonals(kept):
    total = kept[:8]
    for low in range(8, LANES, 8):
        total = total + pltpu.roll(kept[low : low + 8], LANES - low, 1)
    return total


def main_kernel(
    span, scale, feat_hbm, cot_hbm, w_ref, h_ref, skip_ref,
    out_ref, gin_ref, short_ref, long_ref, skip_grad_ref,
    feat_ref, cot_ref, staged, made, grads, zt, gt, rims, mt, gzt, extra, t1_all, lags, lags_rim,
    z_send, g_send, z_rim, g_rim, edge_send, edge_got, edge_ref, head, ahead,
    sums_ref, got_near, part, got_far, full,
    sems, load_sems, near_send, near_recv, far_send, far_recv, near_send2, near_recv2,
):
    rows, channels = cot_ref.shape
    parts = channels // LANES
    groups = h_ref.shape[0]
    blocks = rows // LANES
    f32, bf16 = jnp.float32, jnp.bfloat16
    dps, length = span
    dp, ctx = lax.axis_index("dp"), lax.axis_index("ctx")
    after, before = (dp, (ctx + 1) % length), (dp, (ctx + length - 1) % length)
    near, far = dps * INNER, length // INNER
    outer, inner = ctx // INNER, ctx % INNER
    mine = dp * INNER + inner
    wide = sums_ref.shape[0] // near

    def near_peer(step):
        other = (mine + step) % near
        return other, (other // INNER, outer * INNER + other % INNER)

    def far_peer(step):
        return dp, ((outer + step) % far) * INNER + inner

    has_before = jnp.where(ctx > 0, 1.0, 0.0).astype(f32)
    has_after = jnp.where(ctx + 1 < length, 1.0, 0.0).astype(f32)

    early = rows - LANES - 16
    loads = []
    for source, target in (
        (feat_hbm.at[early:, channels:], feat_ref.at[early:, channels:]),
        (feat_hbm.at[:, :channels], feat_ref.at[:, :channels]),
        (cot_hbm, cot_ref),
        (feat_hbm.at[:early, channels:], feat_ref.at[:early, channels:]),
    ):
        copy = pltpu.make_async_copy(source, target, load_sems.at[len(loads)])
        copy.start()
        loads.append(copy)

    def transfer(source, target, send_sem, recv_sem, device):
        copy = pltpu.make_async_remote_copy(
            src_ref=source, dst_ref=target, send_sem=send_sem, recv_sem=recv_sem,
            device_id=device, device_id_type=pl.DeviceIdType.MESH,
        )
        copy.start()
        return copy

    def send(source, target, index, device):
        return transfer(source, target, sems.at[index], sems.at[index + 1], device)

    peers = [near_peer(step)[1] for step in range(1, near)]
    peers += [far_peer(step) for step in range(1, far)] + [after, before]
    barrier = pltpu.get_barrier_semaphore()
    for peer in peers:
        pl.semaphore_signal(barrier, inc=1, device_id=peer, device_id_type=pl.DeviceIdType.MESH)

    loads[0].wait()
    loads[1].wait()
    edge_send[...] = feat_ref[rows - 16 :, :].astype(f32)[14:16].astype(bf16)
    pl.semaphore_wait(barrier, len(peers))
    edge_copy = send(edge_send, edge_got, 0, after)

    def z_tail(i, _):
        pair = []
        for stream in (1, 2):
            cols = column_tile(stream, i, channels)
            edge = feat_ref[early : early + 16, cols].astype(f32)[14:16]
            pair.append(filtered(feat_ref, w_ref, cols, edge, rows - LANES, LANES))
        z_send[i] = (pair[0] * pair[1]).astype(bf16)
        return 0

    half = parts // 2
    copies = []
    for n in range(2):
        piece = pl.ds(n * half, half)
        lax.fori_loop(n * half, (n + 1) * half, z_tail, 0)
        copies.append(send(z_send.at[piece], z_rim.at[piece], 2 + 2 * n, after))
    edge_copy.wait()
    edge_ref[...] = edge_got[...].astype(f32) * has_before
    loads[2].wait()

    def g_head(i, _):
        own = column_tile(0, i, channels)
        queries = filtered(feat_ref, w_ref, own, edge_ref[:, own], 0, LANES)
        g_send[i] = (cot_ref[:LANES, own].astype(f32) * queries).astype(bf16)
        return 0

    for n in range(2):
        piece = pl.ds(n * half, half)
        lax.fori_loop(n * half, (n + 1) * half, g_head, 0)
        copies.append(send(g_send.at[piece], g_rim.at[piece], 6 + 2 * n, before))
    loads[3].wait()

    def featurize(i, _):
        own = column_tile(0, i, channels)
        for stream in range(3):
            cols = column_tile(stream, i, channels)
            slot = stream * parts + i
            w = w_ref[:, cols]
            staged[slot, 6:8] = edge_ref[:, cols]
            staged[slot, 8:] = feat_ref[:, cols].astype(f32)
            made[slot] = (
                w[0:1] * staged[slot, 8 : 8 + rows]
                + w[1:2] * staged[slot, 7 : 7 + rows]
                + w[2:3] * staged[slot, 6 : 6 + rows]
            )
        total = jnp.zeros((1, LANES), f32)
        for n in range(blocks):
            at = pl.ds(n * LANES, LANES)
            z = (made[parts + i, at] * made[2 * parts + i, at]).astype(bf16).astype(f32)
            g = (cot_ref[at, own].astype(f32) * made[i, at]).astype(bf16).astype(f32)
            total = total + jnp.sum(z * g, axis=0, keepdims=True)
            zt[n, turned_tile(i)] = z.T
            gt[n, turned_tile(i)] = g.T
        sums_ref[pl.ds(groups + i, 1), :] = total
        return 0

    lax.fori_loop(0, parts, featurize, 0)

    s_index = lax.broadcasted_iota(jnp.int32, (LANES, LANES), 0)
    t_index = lax.broadcasted_iota(jnp.int32, (LANES, LANES), 1)
    causal = t_index >= s_index
    contract = lambda a, b, da, db: lax.dot_general(
        a, b, (((da,), (db,)), ((), ())), preferred_element_type=f32
    )

    def convolve(g, _):
        picked = pl.ds(g, parts, stride=PITCH)
        zs = [zt[n, picked].astype(bf16) for n in range(blocks)]
        gs = [gt[n, picked].astype(bf16) for n in range(blocks)]
        none = jnp.zeros((parts, LANES), bf16)
        z_win = jnp.concatenate(
            [jnp.concatenate([a, b], axis=1) for a, b in zip([none] + zs, zs)], axis=0
        )
        g_win = jnp.concatenate(
            [jnp.concatenate([a, b], axis=1) for a, b in zip(gs, gs[1:] + [none])], axis=0
        )
        taps = jnp.broadcast_to(h_ref[pl.ds(g, 1), :].astype(bf16).astype(f32), (LANES, LANES))
        circ = pltpu.roll(taps, 0, 1, stride=1, stride_axis=0)
        t0 = jnp.where(causal, circ, 0.0).astype(bf16)
        t1 = jnp.where(causal, 0.0, circ).astype(bf16)
        t1_all[pl.ds(pl.multiple_of(g * LANES, LANES), LANES)] = t1
        mixed = contract(z_win, jnp.concatenate([t1, t0], axis=0), 1, 0)
        back = contract(g_win, jnp.concatenate([t0, t1], axis=1), 1, 1)
        for n in range(blocks):
            mt[n, picked] = mixed[n * parts : (n + 1) * parts]
            gzt[n, picked] = back[n * parts : (n + 1) * parts]
        prod = contract(z_win, jnp.concatenate(gs, axis=0), 0, 0)
        kept = jnp.where(causal, prod[LANES:], prod[:LANES])
        lags[pl.ds(g, 8, stride=PITCH)] = diagonals(kept)
        return 0

    lax.fori_loop(0, groups, convolve, 0, unroll=8)

    def short_sums(i, stream, n, grad, fresh):
        slot = stream * parts + i
        for tap in range(3):
            low = 8 - tap + n * LANES
            line = pl.ds(groups + parts + (tap * 3 + stream) * parts + i, 1)
            total = jnp.sum(grad * staged[slot, low : low + LANES], axis=0, keepdims=True)
            sums_ref[line, :] = total if fresh else sums_ref[line, :] + total

    def query_part(i, n, fresh, rim):
        own = column_tile(0, i, channels)
        at = pl.ds(n * LANES, LANES)
        q, k, v = made[i, at], made[parts + i, at], made[2 * parts + i, at]
        z = (k * v).astype(bf16).astype(f32)
        mixed = mt[n, turned_tile(i)]
        if rim:
            mixed = mixed + extra[0, turned_tile(i)]
        mixed = mixed.T + skip_ref[:, own] * z
        out_ref[at, own] = (q * mixed).astype(bf16)
        grad = (cot_ref[at, own].astype(f32) * mixed).astype(bf16).astype(f32)
        grads[i, at] = grad
        short_sums(i, 0, n, grad, fresh)

    def pair_part(i, n, fresh, rim):
        own = column_tile(0, i, channels)
        at = pl.ds(n * LANES, LANES)
        q, k, v = made[i, at], made[parts + i, at], made[2 * parts + i, at]
        g = (cot_ref[at, own].astype(f32) * q).astype(bf16).astype(f32)
        grad_z = gzt[n, turned_tile(i)]
        if rim:
            grad_z = grad_z + extra[1, turned_tile(i)]
        grad_z = grad_z.T + skip_ref[:, own] * g
        for stream, other in ((1, v), (2, k)):
            grad = (grad_z * other).astype(bf16).astype(f32)
            grads[stream * parts + i, at] = grad
            short_sums(i, stream, n, grad, fresh)

    def inside(i, _):
        for n in range(1, blocks):
            query_part(i, n, n == 1, False)
        for n in range(blocks - 1):
            pair_part(i, n, n == 0, False)
        return 0

    lax.fori_loop(0, parts, inside, 0)
    for copy in copies:
        copy.wait()

    def turn_rims(i, _):
        rims[0, turned_tile(i)] = (z_rim[i].astype(f32) * has_before).T
        rims[1, turned_tile(i)] = (g_rim[i].astype(f32) * has_after).T
        return 0

    lax.fori_loop(0, parts, turn_rims, 0, unroll=2)

    def convolve_rims(g, _):
        picked = pl.ds(g, parts, stride=PITCH)
        zr = rims[0, picked].astype(bf16)
        gr = rims[1, picked].astype(bf16)
        t1 = t1_all[pl.ds(pl.multiple_of(g * LANES, LANES), LANES)]
        extra[0, picked] = contract(zr, t1, 1, 0)
        extra[1, picked] = contract(gr, t1, 1, 1)
        prod = contract(zr, gt[0, picked].astype(bf16), 0, 0)
        lags_rim[pl.ds(g, 8, stride=PITCH)] = diagonals(jnp.where(causal, 0.0, prod))
        return 0

    lax.fori_loop(0, groups, convolve_rims, 0, unroll=8)
    total = jnp.zeros((groups, LANES), f32)
    for low in range(8):
        at = pl.ds(low * PITCH, groups)
        both = lags[at] + lags_rim[at]
        total = total + (pltpu.roll(both, LANES - low, 1) if low else both)
    sums_ref[:groups] = total

    def rim_part(i, _):
        query_part(i, 0, blocks == 1, True)
        pair_part(i, blocks - 1, blocks == 1, True)
        for stream in range(3):
            head[:, column_tile(stream, i, channels)] = grads[stream * parts + i, 0:2]
        return 0

    lax.fori_loop(0, parts, rim_part, 0)
    used = groups + 10 * parts
    if used < sums_ref.shape[0]:
        sums_ref[used:] = jnp.zeros((sums_ref.shape[0] - used, LANES), f32)

    def share_of(index):
        return pl.ds(pl.multiple_of(index * wide, 8), wide)

    copies = []
    for step in range(1, near):
        other, device = near_peer(step)
        copies.append(transfer(
            sums_ref.at[share_of(other)], got_near.at[step - 1],
            near_send.at[step - 1], near_recv.at[step - 1], device,
        ))
    edge_copy = send(head, ahead, 10, before)

    def adjoint(first, count):
        def one(slot, _):
            cols = pl.ds(pl.multiple_of(slot * LANES, LANES), LANES)
            w = w_ref[:, cols]
            for n in range(first, first + count):
                low = n * LANES
                new = (
                    w[0:1] * grads[slot, low : low + LANES]
                    + w[1:2] * grads[slot, low + 1 : low + 1 + LANES]
                    + w[2:3] * grads[slot, low + 2 : low + 2 + LANES]
                )
                gin_ref[low : low + LANES, cols] = new.astype(bf16)
            return 0

        lax.fori_loop(0, 3 * parts, one, 0)

    adjoint(0, blocks - 1)
    total = sums_ref[share_of(mine)]
    for step, copy in enumerate(copies):
        copy.wait()
        total = total + got_near[step]
    part[...] = total
    copies = [
        transfer(
            part, got_far.at[outer], far_send.at[step - 1], far_recv.at[step - 1], far_peer(step)
        )
        for step in range(1, far)
    ]
    edge_copy.wait()

    def end_rows(slot, _):
        cols = pl.ds(pl.multiple_of(slot * LANES, LANES), LANES)
        grads[slot, rows : rows + 2] = ahead[:, cols] * has_after
        return 0

    lax.fori_loop(0, 3 * parts, end_rows, 0)
    adjoint(blocks - 1, 1)
    got_far[outer] = part[...]
    for copy in copies:
        copy.wait()
    total = got_far[0]
    for step in range(1, far):
        total = total + got_far[step]
    full[share_of(mine)] = total * scale
    copies = [
        transfer(
            full.at[share_of(mine)], full.at[share_of(mine)],
            near_send2.at[step - 1], near_recv2.at[step - 1], near_peer(step)[1],
        )
        for step in range(1, near)
    ]
    for copy in copies:
        copy.wait()
    long_ref[...] = full[:groups]
    for i in range(parts):
        skip_grad_ref[:, i * LANES : (i + 1) * LANES] = full[groups + i : groups + i + 1]
    for tap in range(3):
        for slot in range(3 * parts):
            line = groups + parts + tap * 3 * parts + slot
            short_ref[tap : tap + 1, slot * LANES : (slot + 1) * LANES] = full[line : line + 1]


def body(features, short_w, long_h, skip_bias, cotangent):
    f32, bf16 = jnp.float32, jnp.bfloat16
    feat, cot = features[0], cotangent[0]
    rows, wide = feat.shape
    channels = skip_bias.shape[0]
    parts = channels // LANES
    blocks = rows // LANES
    groups = long_h.shape[0]
    span = (lax.axis_size("dp"), lax.axis_size("ctx"))
    near, far = span[0] * INNER, span[1] // INNER
    used = groups + 10 * parts
    share = -(-used // (8 * near)) * 8
    scale = (span[0] * span[1] * rows) ** (-0.5)
    vmem = pl.BlockSpec(memory_space=pltpu.VMEM)
    hbm = pl.BlockSpec(memory_space=pl.ANY)
    dma = pltpu.SemaphoreType.DMA
    rim = pltpu.VMEM((parts, LANES, LANES), bf16)
    turned = pltpu.VMEM((blocks, turned_rows(channels), LANES), f32)
    turned_pair = pltpu.VMEM((2, turned_rows(channels), LANES), f32)
    output, grad_in, grad_short, grad_long, grad_skip = pl.pallas_call(
        functools.partial(main_kernel, span, scale),
        out_shape=(
            jax.ShapeDtypeStruct((rows, channels), bf16),
            jax.ShapeDtypeStruct((rows, wide), bf16),
            jax.ShapeDtypeStruct((3, wide), f32),
            jax.ShapeDtypeStruct((groups, LANES), f32),
            jax.ShapeDtypeStruct((1, channels), f32),
        ),
        in_specs=[hbm, hbm, vmem, vmem, vmem],
        out_specs=(vmem,) * 5,
        scratch_shapes=[
            pltpu.VMEM((rows, wide), bf16),
            pltpu.VMEM((rows, channels), bf16),
            pltpu.VMEM((3 * parts, rows + 8, LANES), f32),
            pltpu.VMEM((3 * parts, rows, LANES), f32),
            pltpu.VMEM((3 * parts, rows + 8, LANES), f32),
            turned, turned, turned_pair, turned, turned, turned_pair,
            pltpu.VMEM((groups * LANES, LANES), bf16),
            pltpu.VMEM((8 * PITCH, LANES), f32), pltpu.VMEM((8 * PITCH, LANES), f32),
            rim, rim, rim, rim,
            pltpu.VMEM((2, wide), bf16), pltpu.VMEM((2, wide), bf16), pltpu.VMEM((2, wide), f32),
            pltpu.VMEM((2, wide), f32), pltpu.VMEM((2, wide), f32),
            pltpu.VMEM((near * share, LANES), f32),
            pltpu.VMEM((near - 1, share, LANES), f32),
            pltpu.VMEM((share, LANES), f32),
            pltpu.VMEM((far, share, LANES), f32),
            pltpu.VMEM((near * share, LANES), f32),
            dma((12,)), dma((4,)),
            dma((near - 1,)), dma((near - 1,)),
            dma((max(far - 1, 1),)), dma((max(far - 1, 1),)),
            dma((near - 1,)), dma((near - 1,)),
        ],
        compiler_params=pltpu.CompilerParams(
            collective_id=1, has_side_effects=True, vmem_limit_bytes=VMEM_LIMIT
        ),
    )(feat, cot, short_w, long_h, skip_bias[None])
    return output[None], grad_in[None], grad_short, grad_long, grad_skip.reshape(channels)


def solution(mesh):
    return jax.shard_map(
        body,
        mesh=mesh,
        in_specs=(P("dp", "ctx", None), P(), P(), P(), P("dp", "ctx", None)),
        out_specs=(P("dp", "ctx", None), P("dp", "ctx", None), P(), P(), P()),
        check_vma=False,
    )
```

```python
import functools

import jax
import jax.numpy as jnp
from jax import lax
from jax.experimental import pallas as pl
from jax.experimental.pallas import tpu as pltpu
from jax.sharding import PartitionSpec as P

LANES = 128
PITCH = 132
INNER = 4
VMEM_LIMIT = 48 * 1024 * 1024


def delayed(tile, edge, by):
    row = lax.broadcasted_iota(jnp.int32, tile.shape, 0)
    moved = pltpu.roll(tile, by, 0)
    if by == 1:
        return jnp.where(row == 0, edge[1:2], moved)
    return jnp.where(row == 0, edge[0:1], jnp.where(row == 1, edge[1:2], moved))


def filtered(feat_ref, w_ref, cols, edge, first, count):
    w = w_ref[:, cols]
    tile = feat_ref[first : first + count, cols].astype(jnp.float32)
    return w[0:1] * tile + w[1:2] * delayed(tile, edge, 1) + w[2:3] * delayed(tile, edge, 2)


def turned_tile(i):
    return pl.ds(i * PITCH, LANES)


def turned_rows(channels):
    return channels // LANES * PITCH


def column_tile(stream, i, channels):
    return pl.ds(pl.multiple_of(stream * channels + i * LANES, LANES), LANES)


def diagonals(kept):
    total = kept[:8]
    for low in range(8, LANES, 8):
        total = total + pltpu.roll(kept[low : low + 8], LANES - low, 1)
    return total


def main_kernel(
    span, scale, feat_hbm, cot_hbm, w_hbm, h_hbm, skip_hbm,
    out_ref, gin_ref, short_ref, long_ref, skip_grad_ref,
    feat_ref, cot_ref, w_ref, h_ref, skip_ref, staged, made, grads, zt, gt, rims, mt, gzt, extra, t1_all, lags, lags_rim,
    z_send, g_send, z_rim, g_rim, edge_send, edge_got, edge_ref, head, ahead,
    sums_ref, got_near, part, got_far, full,
    sems, load_sems, near_send, near_recv, far_send, far_recv, near_send2, near_recv2,
):
    rows, channels = cot_ref.shape
    parts = channels // LANES
    groups = h_ref.shape[0]
    blocks = rows // LANES
    f32, bf16 = jnp.float32, jnp.bfloat16
    dps, length = span
    dp, ctx = lax.axis_index("dp"), lax.axis_index("ctx")
    after, before = (dp, (ctx + 1) % length), (dp, (ctx + length - 1) % length)
    near, far = dps * INNER, length // INNER
    outer, inner = ctx // INNER, ctx % INNER
    mine = dp * INNER + inner
    wide = sums_ref.shape[0] // near

    def near_peer(step):
        other = (mine + step) % near
        return other, (other // INNER, outer * INNER + other % INNER)

    def far_peer(step):
        return dp, ((outer + step) % far) * INNER + inner

    has_before = jnp.where(ctx > 0, 1.0, 0.0).astype(f32)
    has_after = jnp.where(ctx + 1 < length, 1.0, 0.0).astype(f32)

    early = rows - LANES - 16
    loads = []
    for source, target in (
        (feat_hbm.at[early:, channels:], feat_ref.at[early:, channels:]),
        (w_hbm, w_ref),
        (feat_hbm.at[:, :channels], feat_ref.at[:, :channels]),
        (cot_hbm, cot_ref),
        (feat_hbm.at[:early, channels:], feat_ref.at[:early, channels:]),
        (h_hbm, h_ref),
        (skip_hbm, skip_ref),
    ):
        copy = pltpu.make_async_copy(source, target, load_sems.at[len(loads)])
        copy.start()
        loads.append(copy)

    def transfer(source, target, send_sem, recv_sem, device):
        copy = pltpu.make_async_remote_copy(
            src_ref=source, dst_ref=target, send_sem=send_sem, recv_sem=recv_sem,
            device_id=device, device_id_type=pl.DeviceIdType.MESH,
        )
        copy.start()
        return copy

    def send(source, target, index, device):
        return transfer(source, target, sems.at[index], sems.at[index + 1], device)

    peers = [near_peer(step)[1] for step in range(1, near)]
    peers += [far_peer(step) for step in range(1, far)] + [after, before]
    barrier = pltpu.get_barrier_semaphore()
    for peer in peers:
        pl.semaphore_signal(barrier, inc=1, device_id=peer, device_id_type=pl.DeviceIdType.MESH)

    for load in loads[:3]:
        load.wait()
    edge_send[...] = feat_ref[rows - 16 :, :].astype(f32)[14:16].astype(bf16)
    pl.semaphore_wait(barrier, len(peers))
    edge_copy = send(edge_send, edge_got, 0, after)

    def z_tail(i, _):
        pair = []
        for stream in (1, 2):
            cols = column_tile(stream, i, channels)
            edge = feat_ref[early : early + 16, cols].astype(f32)[14:16]
            pair.append(filtered(feat_ref, w_ref, cols, edge, rows - LANES, LANES))
        z_send[i] = (pair[0] * pair[1]).astype(bf16)
        return 0

    half = parts // 2
    copies = []
    for n in range(2):
        piece = pl.ds(n * half, half)
        lax.fori_loop(n * half, (n + 1) * half, z_tail, 0)
        copies.append(send(z_send.at[piece], z_rim.at[piece], 2 + 2 * n, after))
    edge_copy.wait()
    edge_ref[...] = edge_got[...].astype(f32) * has_before
    loads[3].wait()

    def g_head(i, _):
        own = column_tile(0, i, channels)
        queries = filtered(feat_ref, w_ref, own, edge_ref[:, own], 0, LANES)
        g_send[i] = (cot_ref[:LANES, own].astype(f32) * queries).astype(bf16)
        return 0

    for n in range(2):
        piece = pl.ds(n * half, half)
        lax.fori_loop(n * half, (n + 1) * half, g_head, 0)
        copies.append(send(g_send.at[piece], g_rim.at[piece], 6 + 2 * n, before))
    for load in loads[4:]:
        load.wait()

    def featurize(i, _):
        own = column_tile(0, i, channels)
        for stream in range(3):
            cols = column_tile(stream, i, channels)
            slot = stream * parts + i
            w = w_ref[:, cols]
            staged[slot, 6:8] = edge_ref[:, cols]
            staged[slot, 8:] = feat_ref[:, cols].astype(f32)
            made[slot] = (
                w[0:1] * staged[slot, 8 : 8 + rows]
                + w[1:2] * staged[slot, 7 : 7 + rows]
                + w[2:3] * staged[slot, 6 : 6 + rows]
            )
        total = jnp.zeros((1, LANES), f32)
        for n in range(blocks):
            at = pl.ds(n * LANES, LANES)
            z = (made[parts + i, at] * made[2 * parts + i, at]).astype(bf16).astype(f32)
            g = (cot_ref[at, own].astype(f32) * made[i, at]).astype(bf16).astype(f32)
            total = total + jnp.sum(z * g, axis=0, keepdims=True)
            zt[n, turned_tile(i)] = z.T
            gt[n, turned_tile(i)] = g.T
        sums_ref[pl.ds(groups + i, 1), :] = total
        return 0

    lax.fori_loop(0, parts, featurize, 0)

    s_index = lax.broadcasted_iota(jnp.int32, (LANES, LANES), 0)
    t_index = lax.broadcasted_iota(jnp.int32, (LANES, LANES), 1)
    causal = t_index >= s_index
    contract = lambda a, b, da, db: lax.dot_general(
        a, b, (((da,), (db,)), ((), ())), preferred_element_type=f32
    )

    def convolve(g, _):
        picked = pl.ds(g, parts, stride=PITCH)
        zs = [zt[n, picked].astype(bf16) for n in range(blocks)]
        gs = [gt[n, picked].astype(bf16) for n in range(blocks)]
        none = jnp.zeros((parts, LANES), bf16)
        z_win = jnp.concatenate(
            [jnp.concatenate([a, b], axis=1) for a, b in zip([none] + zs, zs)], axis=0
        )
        g_win = jnp.concatenate(
            [jnp.concatenate([a, b], axis=1) for a, b in zip(gs, gs[1:] + [none])], axis=0
        )
        taps = jnp.broadcast_to(h_ref[pl.ds(g, 1), :].astype(bf16).astype(f32), (LANES, LANES))
        circ = pltpu.roll(taps, 0, 1, stride=1, stride_axis=0)
        t0 = jnp.where(causal, circ, 0.0).astype(bf16)
        t1 = jnp.where(causal, 0.0, circ).astype(bf16)
        t1_all[pl.ds(pl.multiple_of(g * LANES, LANES), LANES)] = t1
        mixed = contract(z_win, jnp.concatenate([t1, t0], axis=0), 1, 0)
        back = contract(g_win, jnp.concatenate([t0, t1], axis=1), 1, 1)
        for n in range(blocks):
            mt[n, picked] = mixed[n * parts : (n + 1) * parts]
            gzt[n, picked] = back[n * parts : (n + 1) * parts]
        prod = contract(z_win, jnp.concatenate(gs, axis=0), 0, 0)
        kept = jnp.where(causal, prod[LANES:], prod[:LANES])
        lags[pl.ds(g, 8, stride=PITCH)] = diagonals(kept)
        return 0

    lax.fori_loop(0, groups, convolve, 0, unroll=8)

    def short_sums(i, stream, n, grad, fresh):
        slot = stream * parts + i
        for tap in range(3):
            low = 8 - tap + n * LANES
            line = pl.ds(groups + parts + (tap * 3 + stream) * parts + i, 1)
            total = jnp.sum(grad * staged[slot, low : low + LANES], axis=0, keepdims=True)
            sums_ref[line, :] = total if fresh else sums_ref[line, :] + total

    def query_part(i, n, fresh, rim):
        own = column_tile(0, i, channels)
        at = pl.ds(n * LANES, LANES)
        q, k, v = made[i, at], made[parts + i, at], made[2 * parts + i, at]
        z = (k * v).astype(bf16).astype(f32)
        mixed = mt[n, turned_tile(i)]
        if rim:
            mixed = mixed + extra[0, turned_tile(i)]
        mixed = mixed.T + skip_ref[:, own] * z
        out_ref[at, own] = (q * mixed).astype(bf16)
        grad = (cot_ref[at, own].astype(f32) * mixed).astype(bf16).astype(f32)
        grads[i, at] = grad
        short_sums(i, 0, n, grad, fresh)

    def pair_part(i, n, fresh, rim):
        own = column_tile(0, i, channels)
        at = pl.ds(n * LANES, LANES)
        q, k, v = made[i, at], made[parts + i, at], made[2 * parts + i, at]
        g = (cot_ref[at, own].astype(f32) * q).astype(bf16).astype(f32)
        grad_z = gzt[n, turned_tile(i)]
        if rim:
            grad_z = grad_z + extra[1, turned_tile(i)]
        grad_z = grad_z.T + skip_ref[:, own] * g
        for stream, other in ((1, v), (2, k)):
            grad = (grad_z * other).astype(bf16).astype(f32)
            grads[stream * parts + i, at] = grad
            short_sums(i, stream, n, grad, fresh)

    def inside(i, _):
        for n in range(1, blocks):
            query_part(i, n, n == 1, False)
        for n in range(blocks - 1):
            pair_part(i, n, n == 0, False)
        return 0

    lax.fori_loop(0, parts, inside, 0)
    for copy in copies:
        copy.wait()

    def turn_rims(i, _):
        rims[0, turned_tile(i)] = (z_rim[i].astype(f32) * has_before).T
        rims[1, turned_tile(i)] = (g_rim[i].astype(f32) * has_after).T
        return 0

    lax.fori_loop(0, parts, turn_rims, 0, unroll=2)

    def convolve_rims(g, _):
        picked = pl.ds(g, parts, stride=PITCH)
        zr = rims[0, picked].astype(bf16)
        gr = rims[1, picked].astype(bf16)
        t1 = t1_all[pl.ds(pl.multiple_of(g * LANES, LANES), LANES)]
        extra[0, picked] = contract(zr, t1, 1, 0)
        extra[1, picked] = contract(gr, t1, 1, 1)
        prod = contract(zr, gt[0, picked].astype(bf16), 0, 0)
        lags_rim[pl.ds(g, 8, stride=PITCH)] = diagonals(jnp.where(causal, 0.0, prod))
        return 0

    lax.fori_loop(0, groups, convolve_rims, 0, unroll=16)
    total = jnp.zeros((groups, LANES), f32)
    for low in range(8):
        at = pl.ds(low * PITCH, groups)
        both = lags[at] + lags_rim[at]
        total = total + (pltpu.roll(both, LANES - low, 1) if low else both)
    sums_ref[:groups] = total

    def rim_part(i, _):
        query_part(i, 0, blocks == 1, True)
        pair_part(i, blocks - 1, blocks == 1, True)
        for stream in range(3):
            head[:, column_tile(stream, i, channels)] = grads[stream * parts + i, 0:2]
        return 0

    lax.fori_loop(0, parts, rim_part, 0)
    used = groups + 10 * parts
    if used < sums_ref.shape[0]:
        sums_ref[used:] = jnp.zeros((sums_ref.shape[0] - used, LANES), f32)

    def share_of(index):
        return pl.ds(pl.multiple_of(index * wide, 8), wide)

    copies = []
    for step in range(1, near):
        other, device = near_peer(step)
        copies.append(transfer(
            sums_ref.at[share_of(other)], got_near.at[step - 1],
            near_send.at[step - 1], near_recv.at[step - 1], device,
        ))
    edge_copy = send(head, ahead, 10, before)

    def adjoint(first, count):
        def one(slot, _):
            cols = pl.ds(pl.multiple_of(slot * LANES, LANES), LANES)
            w = w_ref[:, cols]
            for n in range(first, first + count):
                low = n * LANES
                new = (
                    w[0:1] * grads[slot, low : low + LANES]
                    + w[1:2] * grads[slot, low + 1 : low + 1 + LANES]
                    + w[2:3] * grads[slot, low + 2 : low + 2 + LANES]
                )
                gin_ref[low : low + LANES, cols] = new.astype(bf16)
            return 0

        lax.fori_loop(0, 3 * parts, one, 0)

    adjoint(0, blocks - 1)
    total = sums_ref[share_of(mine)]
    for step, copy in enumerate(copies):
        copy.wait()
        total = total + got_near[step]
    part[...] = total
    copies = [
        transfer(
            part, got_far.at[outer], far_send.at[step - 1], far_recv.at[step - 1], far_peer(step)
        )
        for step in range(1, far)
    ]
    edge_copy.wait()

    def end_rows(slot, _):
        cols = pl.ds(pl.multiple_of(slot * LANES, LANES), LANES)
        grads[slot, rows : rows + 2] = ahead[:, cols] * has_after
        return 0

    lax.fori_loop(0, 3 * parts, end_rows, 0)
    adjoint(blocks - 1, 1)
    got_far[outer] = part[...]
    for copy in copies:
        copy.wait()
    total = got_far[0]
    for step in range(1, far):
        total = total + got_far[step]
    full[share_of(mine)] = total * scale
    copies = [
        transfer(
            full.at[share_of(mine)], full.at[share_of(mine)],
            near_send2.at[step - 1], near_recv2.at[step - 1], near_peer(step)[1],
        )
        for step in range(1, near)
    ]
    for copy in copies:
        copy.wait()
    long_ref[...] = full[:groups]
    for i in range(parts):
        skip_grad_ref[:, i * LANES : (i + 1) * LANES] = full[groups + i : groups + i + 1]
    for tap in range(3):
        for slot in range(3 * parts):
            line = groups + parts + tap * 3 * parts + slot
            short_ref[tap : tap + 1, slot * LANES : (slot + 1) * LANES] = full[line : line + 1]


def store_kernel(*refs):
    sems = refs[10]
    copies = [pltpu.make_async_copy(refs[n], refs[5 + n], sems.at[n]) for n in range(5)]
    for copy in copies:
        copy.start()
    for copy in copies:
        copy.wait()


def body(features, short_w, long_h, skip_bias, cotangent):
    f32, bf16 = jnp.float32, jnp.bfloat16
    feat, cot = features[0], cotangent[0]
    rows, wide = feat.shape
    channels = skip_bias.shape[0]
    parts = channels // LANES
    blocks = rows // LANES
    groups = long_h.shape[0]
    span = (lax.axis_size("dp"), lax.axis_size("ctx"))
    near, far = span[0] * INNER, span[1] // INNER
    used = groups + 10 * parts
    share = -(-used // (8 * near)) * 8
    scale = (span[0] * span[1] * rows) ** (-0.5)
    vmem = pl.BlockSpec(memory_space=pltpu.VMEM)
    hbm = pl.BlockSpec(memory_space=pltpu.HBM)
    dma = pltpu.SemaphoreType.DMA
    rim = pltpu.VMEM((parts, LANES, LANES), bf16)
    turned = pltpu.VMEM((blocks, turned_rows(channels), LANES), f32)
    turned_pair = pltpu.VMEM((2, turned_rows(channels), LANES), f32)
    results = pl.pallas_call(
        functools.partial(main_kernel, span, scale),
        out_shape=(
            jax.ShapeDtypeStruct((rows, channels), bf16),
            jax.ShapeDtypeStruct((rows, wide), bf16),
            jax.ShapeDtypeStruct((3, wide), f32),
            jax.ShapeDtypeStruct((groups, LANES), f32),
            jax.ShapeDtypeStruct((1, channels), f32),
        ),
        in_specs=[hbm] * 5,
        out_specs=(vmem,) * 5,
        scratch_shapes=[
            pltpu.VMEM((rows, wide), bf16),
            pltpu.VMEM((rows, channels), bf16),
            pltpu.VMEM(short_w.shape, f32),
            pltpu.VMEM(long_h.shape, f32),
            pltpu.VMEM((1, channels), f32),
            pltpu.VMEM((3 * parts, rows + 8, LANES), f32),
            pltpu.VMEM((3 * parts, rows, LANES), f32),
            pltpu.VMEM((3 * parts, rows + 8, LANES), f32),
            turned, turned, turned_pair, turned, turned, turned_pair,
            pltpu.VMEM((groups * LANES, LANES), bf16),
            pltpu.VMEM((8 * PITCH, LANES), f32), pltpu.VMEM((8 * PITCH, LANES), f32),
            rim, rim, rim, rim,
            pltpu.VMEM((2, wide), bf16), pltpu.VMEM((2, wide), bf16), pltpu.VMEM((2, wide), f32),
            pltpu.VMEM((2, wide), f32), pltpu.VMEM((2, wide), f32),
            pltpu.VMEM((near * share, LANES), f32),
            pltpu.VMEM((near - 1, share, LANES), f32),
            pltpu.VMEM((share, LANES), f32),
            pltpu.VMEM((far, share, LANES), f32),
            pltpu.VMEM((near * share, LANES), f32),
            dma((12,)), dma((7,)),
            dma((near - 1,)), dma((near - 1,)),
            dma((max(far - 1, 1),)), dma((max(far - 1, 1),)),
            dma((near - 1,)), dma((near - 1,)),
        ],
        compiler_params=pltpu.CompilerParams(
            collective_id=1, has_side_effects=True, vmem_limit_bytes=VMEM_LIMIT
        ),
    )(feat, cot, short_w, long_h, skip_bias[None])
    output, grad_in, grad_short, grad_long, grad_skip = pl.pallas_call(
        store_kernel,
        out_shape=tuple(jax.ShapeDtypeStruct(r.shape, r.dtype) for r in results),
        in_specs=[vmem] * 5,
        out_specs=(hbm,) * 5,
        scratch_shapes=[dma((5,))],
        compiler_params=pltpu.CompilerParams(vmem_limit_bytes=1024 * 1024),
    )(*results)
    return output[None], grad_in[None], grad_short, grad_long, grad_skip.reshape(channels)


def solution(mesh):
    return jax.shard_map(
        body,
        mesh=mesh,
        in_specs=(P("dp", "ctx", None), P(), P(), P(), P("dp", "ctx", None)),
        out_specs=(P("dp", "ctx", None), P("dp", "ctx", None), P(), P(), P()),
        check_vma=False,
    )
```
